32 devices in a mesh: gz: 16 (over z, y, x), col: 2 (over core).
Axes of the slice: x: 2, y: 2, z: 4, core: 2. Of those that a mesh axis runs over, the one named last changes fastest.
Arguments:
- velocity: float32 [64, 3, 128, 128], P('gz', None, 'col'), may hold values from -6 to 6
- forces: float32 [3, 131072], P(None, ('gz', 'col')), may hold values from -60 to 60
- offsets: float32 [3, 131072], P(None, ('gz', 'col')), may hold values from 0 to 1
- cell_x: int32 [131072], P(('gz', 'col')), may hold values from 0 to 127
- cell_y: int32 [131072], P(('gz', 'col')), may hold values from 0 to 127
- cell_z: int32 [131072], P(('gz', 'col')), may hold values from 0 to 12
- band_start: int32 [16], P('gz'), may hold values from 0 to 15, as said below
Outputs:
- force_field: float32 [64, 3, 128, 128], P('gz', None, 'col')
- velocity_next: float32 [64, 3, 128, 128], P('gz', None, 'col')
The draws below stay inside these ranges and needn't reach their ends.
Inputs may be any that keep to these rules, and one draw needn't show every extreme that they name: (g - band_start[g]) mod 16 lies in 0 to 3 for every gz index g.
All inputs are finite; a program needn't handle non-finite values.
Results may differ from the reference program's by a relative error of at most 0.0037.
Values sent between devices are 32-bit elements; how exact they have to be, the bound alone decides.
A program may use at most 64 MiB of HBM per device.

```python
import jax
import jax.numpy as jnp
from jax import lax

CZ = 4
NX = 128
NY = 128
MK_DEV = 4096
BAND = 4
BANDZ = 16
NZ = 64
MARKERS = 131072
N_GZ = 16
N_COL = 2


def draw_band_start(key, part):
    backward = jax.random.randint(key, (N_GZ,), 0, BAND)
    backward = backward.at[0].set(0).at[1].set(BAND - 1)
    return ((jnp.arange(N_GZ, dtype=jnp.int32) - backward) % N_GZ).astype(jnp.int32)


def with_ends(entries, key, smallest, high):
    spot = [jax.random.randint(jax.random.fold_in(key, axis), (), 0, length) for axis, length in enumerate(entries.shape)]
    longest = entries.shape.index(max(entries.shape))
    next_to = spot[:longest] + [(spot[longest] + 1) % entries.shape[longest]] + spot[longest + 1:]
    return entries.at[tuple(spot)].set(smallest).at[tuple(next_to)].set(high)


def levels(own_key, extent, shards, least, largest):
    factor_of, own = 1.0, jax.random.fold_in(own_key, 6)
    for position, shards_of in shards:
        steps = jnp.exp(jax.random.uniform(jax.random.fold_in(own, position), (shards_of,), jnp.float32, least / len(shards), largest / len(shards)))
        factor_of = factor_of * jnp.repeat(steps, extent[position] // shards_of).reshape([-1 if axis == position else 1 for axis in range(len(extent))])
    return factor_of


def normal_values(rng, dims, scale, reach, cuts=(), held_as=jnp.bfloat16):
    result = jax.random.normal(rng, dims, jnp.float32) * scale
    if len(cuts) > 0:
        result = levels(rng, dims, cuts, -0.22, 0.18) * result
    return jnp.clip(result, min=-reach, max=reach).astype(held_as)


def setup_inputs(seed: int = 0) -> dict:
    arg_keys = jax.random.split(jax.random.key(seed), 8)
    velocity = normal_values(arg_keys[0], (NZ, 3, NX, NY), 1.0, 6.0, ((0, 16), (2, 2)), jnp.float32)
    forces = normal_values(arg_keys[1], (3, MARKERS), 10.0, 60.0, ((1, 32),), jnp.float32)
    offsets = jnp.clip(1.0 * jax.random.uniform(arg_keys[2], (3, MARKERS), jnp.float32) ** levels(arg_keys[2], (3, MARKERS), ((1, 32),), -0.2, 0.2), 0.0, 1.0)
    cell_x = with_ends(jax.random.randint(arg_keys[3], (MARKERS,), 0, NX), jax.random.fold_in(arg_keys[3], 1), 0, NX - 1).astype(jnp.int32)
    cell_y = with_ends(jax.random.randint(arg_keys[4], (MARKERS,), 0, NY), jax.random.fold_in(arg_keys[4], 1), 0, NY - 1).astype(jnp.int32)
    cell_z = with_ends(jax.random.randint(arg_keys[5], (MARKERS,), 0, BANDZ - 3), jax.random.fold_in(arg_keys[5], 1), 0, (BANDZ - 3) - 1).astype(jnp.int32)
    band_start = draw_band_start(jax.random.fold_in(arg_keys[7], 71), 0)
    return dict(velocity=velocity, forces=forces, offsets=offsets, cell_x=cell_x, cell_y=cell_y, cell_z=cell_z, band_start=band_start)


def delta_weights(fraction):
    root_term = jnp.sqrt(1.0 + 4.0 * fraction - 4.0 * fraction * fraction)
    return jnp.stack([(3.0 - 2.0 * fraction - root_term) / 8.0, (3.0 - 2.0 * fraction + root_term) / 8.0, (1.0 + 2.0 * fraction + root_term) / 8.0, (1.0 + 2.0 * fraction - root_term) / 8.0])

def reference(velocity, forces, offsets, cell_x, cell_y, cell_z, band_start):
    owners = jnp.repeat(band_start, MK_DEV * N_COL)
    z_base = owners * CZ + cell_z
    x_weights = delta_weights(offsets[0])
    y_weights = delta_weights(offsets[1]).T
    z_weights = delta_weights(offsets[2])
    y_rounded = lax.optimization_barrier(y_weights.astype(jnp.bfloat16)).astype(jnp.float32)
    y_index = jnp.stack([(cell_y + corner) % NY for corner in range(4)], axis=1).astype(jnp.int32)
    components = jnp.arange(3, dtype=jnp.int32)
    force_t = forces.T
    field = jnp.zeros((NZ, 3, NX, NY), jnp.float32)
    for z_corner in range(4):
        z_index = ((z_base + z_corner) % NZ).astype(jnp.int32)
        for x_corner in range(4):
            x_index = ((cell_x + x_corner) % NX).astype(jnp.int32)
            scaled = z_weights[z_corner][:, None] * force_t * x_weights[x_corner][:, None]
            scaled = lax.optimization_barrier(scaled.astype(jnp.bfloat16)).astype(jnp.float32)
            values = scaled[:, :, None] * y_rounded[:, None, :]
            field = field.at[z_index[:, None, None], components[None, :, None], x_index[:, None, None], y_index[:, None, :]].add(values)
    neighbours = jnp.roll(velocity, 1, 0) + jnp.roll(velocity, -1, 0)
    neighbours = neighbours + jnp.roll(velocity, 1, 2) + jnp.roll(velocity, -1, 2)
    neighbours = neighbours + jnp.roll(velocity, 1, 3) + jnp.roll(velocity, -1, 3)
    velocity_next = velocity + 0.15 * (neighbours - 6.0 * velocity) + field
    return (field, velocity_next)
```

```python
import functools

import jax
import jax.numpy as jnp
from jax import lax
from jax.experimental import pallas as pl
from jax.experimental.pallas import tpu as pltpu
from jax.sharding import PartitionSpec as P

BAND = 4
CORNERS = 4
VISCOUS = 0.15
LANES = 128
SUBLANES = 8
GROUPS = 4
MESH = pl.DeviceIdType.MESH


def delta_weights(fraction):
    root_term = jnp.sqrt(1.0 + 4.0 * fraction - 4.0 * fraction * fraction)
    return (
        (3.0 - 2.0 * fraction - root_term) / 8.0,
        (3.0 - 2.0 * fraction + root_term) / 8.0,
        (1.0 + 2.0 * fraction + root_term) / 8.0,
        (1.0 + 2.0 * fraction - root_term) / 8.0,
    )


def pick(distance, weights):
    result = jnp.where(distance == 0, weights[0], 0.0)
    for corner in range(1, CORNERS):
        result = jnp.where(distance == corner, weights[corner], result)
    return result


def wrapped(distance, period):
    if period & (period - 1) == 0:
        return distance & (period - 1)
    return jnp.where(distance < 0, distance + period, distance)


def kernel(
    sizes,
    packed_ref,
    velocity_ref,
    field_ref,
    next_ref,
    markers,
    left,
    right,
    total,
    outgoing,
    incoming,
    z_halo,
    x_halo,
    send_sems,
    recv_sems,
):
    gz_count, col_count, slab_depth, half_x, width_y, rows_each = sizes
    full_x = half_x * col_count
    full_z = slab_depth * gz_count
    group_x = full_x // GROUPS
    local_x = group_x + SUBLANES
    gz = lax.axis_index("gz")
    col = lax.axis_index("col")
    steps = [by for reach in range(1, BAND) for by in (reach, -reach)]

    def gz_at(by):
        return lax.rem(gz + (by + gz_count), gz_count)

    other_col = lax.rem(col + 1, col_count)

    barrier = pltpu.get_barrier_semaphore()
    for by in steps:
        pl.semaphore_signal(barrier, inc=1, device_id={"gz": gz_at(by)}, device_id_type=MESH)
    pl.semaphore_signal(barrier, inc=1, device_id={"col": other_col}, device_id_type=MESH)
    pl.semaphore_wait(barrier, len(steps) + 1)

    copies = []

    def send(source, target, slot, device):
        copy = pltpu.make_async_remote_copy(
            src_ref=source,
            dst_ref=target,
            send_sem=send_sems.at[slot],
            recv_sem=recv_sems.at[slot],
            device_id=device,
            device_id_type=MESH,
        )
        copy.start()
        copies.append(copy)
        return copy

    for slot, by in enumerate(steps):
        send(packed_ref, markers.at[slot + 1], slot + 1, {"gz": gz_at(by)})
    base = len(steps) + 1
    halos = [
        send(velocity_ref.at[slab_depth - 1], z_halo.at[0], base, {"gz": gz_at(1)}),
        send(velocity_ref.at[0], z_halo.at[1], base + 1, {"gz": gz_at(-1)}),
        send(
            velocity_ref.at[:, :, half_x - SUBLANES : half_x],
            x_halo.at[0],
            base + 2,
            {"col": other_col},
        ),
        send(velocity_ref.at[:, :, 0:SUBLANES], x_halo.at[1], base + 3, {"col": other_col}),
    ]

    markers[0] = packed_ref[...]
    total[...] = jnp.zeros_like(total)

    first_x = col * half_x
    first_z = gz * slab_depth
    pieces = rows_each // SUBLANES
    y_rows = lax.broadcasted_iota(jnp.int32, (width_y, LANES), 0)
    x_rows = lax.broadcasted_iota(jnp.int32, (local_x, LANES), 0)

    def fill(source, piece):
        start = pl.multiple_of(piece * SUBLANES, SUBLANES)

        def param(index):
            return markers[source, pl.ds(index * rows_each + start, SUBLANES), :]

        forces = [param(c) for c in range(3)]
        wx = delta_weights(param(3))
        wy = delta_weights(param(4))
        wz = delta_weights(param(5))
        x_rel = wrapped(param(6).astype(jnp.int32) - first_x, full_x)
        y_cell = param(7).astype(jnp.int32)
        z_cell = param(8).astype(jnp.int32)
        group = x_rel // group_x
        x_local = x_rel - group * group_x
        members = [jnp.where(group == g, 1.0, 0.0) for g in range(GROUPS)]
        scaled = []
        for plane in range(slab_depth):
            z_weight = pick(wrapped(plane + first_z - z_cell, full_z), wz)
            scaled.extend(z_weight * force for force in forces)
        for row in range(SUBLANES):
            lanes = slice(row * LANES, (row + 1) * LANES)

            def line(value):
                return value[row : row + 1, :]

            y_hits = pick(
                wrapped(y_rows - line(y_cell), width_y), [line(w) for w in wy]
            ).astype(jnp.bfloat16)
            for g in range(GROUPS):
                member = jnp.broadcast_to(line(members[g]), (width_y, LANES)).astype(jnp.bfloat16)
                right[g * width_y : (g + 1) * width_y, lanes] = y_hits * member
            x_hits = pick(x_rows - line(x_local), [line(w) for w in wx])
            for pair in range(len(scaled) // 2):
                both = jnp.concatenate(
                    [line(scaled[2 * pair]) * x_hits, line(scaled[2 * pair + 1]) * x_hits], axis=0
                )
                left[2 * pair * local_x : 2 * (pair + 1) * local_x, lanes] = both.astype(jnp.bfloat16)

    def one_source(source, _):
        @pl.when(source > 0)
        def _():
            pltpu.make_async_remote_copy(
                src_ref=packed_ref,
                dst_ref=markers.at[source],
                send_sem=send_sems.at[source],
                recv_sem=recv_sems.at[source],
                device_id={"gz": gz_at(1)},
                device_id_type=MESH,
            ).wait_recv()

        def one_piece(piece, _):
            fill(source, piece)
            total[...] += lax.dot_general(
                left[...],
                right[...],
                (((1,), (1,)), ((), ())),
                preferred_element_type=jnp.float32,
            )
            return 0

        lax.fori_loop(0, pieces, one_piece, 0)
        return 0

    lax.fori_loop(0, len(steps) + 1, one_source, 0)

    own_groups = GROUPS // col_count

    def gathered(plane, component, group):
        start = (plane * 3 + component) * local_x
        main = total[start : start + group_x, group * width_y : (group + 1) * width_y]
        before = (group - 1) % GROUPS
        spill = total[
            start + group_x : start + local_x, before * width_y : (before + 1) * width_y
        ]
        return main, spill

    def put(target, plane, component, group, place):
        main, spill = gathered(plane, component, group)
        start = place * group_x
        target[plane, component, start : start + SUBLANES, :] = main[:SUBLANES] + spill
        target[plane, component, start + SUBLANES : start + group_x, :] = main[SUBLANES:]

    for plane in range(slab_depth):
        for component in range(3):
            for place in range(own_groups):
                put(outgoing, plane, component, own_groups + place, place)
    exchange = send(outgoing, incoming, base + 4, {"col": other_col})

    for halo in halos:
        halo.wait_recv()
    x_index = lax.broadcasted_iota(jnp.int32, (half_x, width_y), 0)
    for plane in range(slab_depth):
        for component in range(3):
            for place in range(own_groups):
                put(field_ref, plane, component, place, place)
            here = velocity_ref[plane, component]
            below = z_halo[0, component] if plane == 0 else velocity_ref[plane - 1, component]
            above = (
                z_halo[1, component]
                if plane == slab_depth - 1
                else velocity_ref[plane + 1, component]
            )
            low = x_halo[0, plane, component, SUBLANES - 1 : SUBLANES, :]
            high = x_halo[1, plane, component, 0:1, :]
            x_low = jnp.where(x_index == 0, low, pltpu.roll(here, 1, 0))
            x_high = jnp.where(x_index == half_x - 1, high, pltpu.roll(here, half_x - 1, 0))
            near = above + below + x_low + x_high
            near = near + pltpu.roll(here, 1, 1) + pltpu.roll(here, width_y - 1, 1)
            next_ref[plane, component] = here + VISCOUS * (near - 6.0 * here)

    exchange.wait_recv()
    for plane in range(slab_depth):
        for component in range(3):
            own = field_ref[plane, component] + incoming[plane, component]
            field_ref[plane, component] = own
            next_ref[plane, component] = next_ref[plane, component] + own
    for copy in copies:
        copy.wait_send()


def on_device(sizes, velocity, forces, offsets, cell_x, cell_y, cell_z, band_start):
    gz_count, col_count, slab_depth, half_x, width_y, rows_each = sizes
    full_x = half_x * col_count
    full_z = slab_depth * gz_count
    z_cell = (band_start[0] * slab_depth + cell_z) % full_z
    cells = jnp.stack([cell_x, cell_y, z_cell]).astype(jnp.float32)
    packed = jnp.concatenate([forces, offsets, cells], axis=0).reshape(9 * rows_each, LANES)
    sources = 2 * BAND - 1
    local_x = full_x // GROUPS + SUBLANES
    left_rows = slab_depth * 3 * local_x
    right_rows = GROUPS * width_y
    block = SUBLANES * LANES
    shape = jax.ShapeDtypeStruct(velocity.shape, jnp.float32)
    copies = sources + 5
    return pl.pallas_call(
        functools.partial(kernel, sizes),
        out_shape=(shape, shape),
        in_specs=[pl.BlockSpec(memory_space=pltpu.VMEM)] * 2,
        out_specs=(pl.BlockSpec(memory_space=pltpu.VMEM),) * 2,
        scratch_shapes=[
            pltpu.VMEM((sources, 9 * rows_each, LANES), jnp.float32),
            pltpu.VMEM((left_rows, block), jnp.bfloat16),
            pltpu.VMEM((right_rows, block), jnp.bfloat16),
            pltpu.VMEM((left_rows, right_rows), jnp.float32),
            pltpu.VMEM(velocity.shape, jnp.float32),
            pltpu.VMEM(velocity.shape, jnp.float32),
            pltpu.VMEM((2,) + velocity.shape[1:], jnp.float32),
            pltpu.VMEM((2, slab_depth, 3, SUBLANES, width_y), jnp.float32),
            pltpu.SemaphoreType.DMA((copies,)),
            pltpu.SemaphoreType.DMA((copies,)),
        ],
        compiler_params=pltpu.CompilerParams(
            collective_id=0, has_side_effects=True, vmem_limit_bytes=48 * 1024 * 1024
        ),
    )(packed, velocity)


def solution(mesh):
    from_shapes = functools.partial(sized, mesh)
    in_specs = (
        P("gz", None, "col", None),
        P(None, ("gz", "col")),
        P(None, ("gz", "col")),
        P(("gz", "col")),
        P(("gz", "col")),
        P(("gz", "col")),
        P("gz"),
    )
    out_specs = (P("gz", None, "col", None), P("gz", None, "col", None))
    return jax.shard_map(
        from_shapes, mesh=mesh, in_specs=in_specs, out_specs=out_specs, check_vma=False
    )


def sized(mesh, velocity, forces, offsets, cell_x, cell_y, cell_z, band_start):
    slab_depth, _, half_x, width_y = velocity.shape
    rows_each = cell_x.shape[0] // LANES
    sizes = (mesh.shape["gz"], mesh.shape["col"], slab_depth, half_x, width_y, rows_each)
    return on_device(sizes, velocity, forces, offsets, cell_x, cell_y, cell_z, band_start)
```

```python
import functools

import jax
import jax.numpy as jnp
from jax import lax
from jax.experimental import pallas as pl
from jax.experimental.pallas import tpu as pltpu
from jax.sharding import PartitionSpec as P

BAND = 4
CORNERS = 4
VISCOUS = 0.15
LANES = 128
SUBLANES = 8
PIECE_ROWS = 32
GROUPS = 4
MESH = pl.DeviceIdType.MESH


def delta_weights(fraction):
    root_term = jnp.sqrt(1.0 + 4.0 * fraction - 4.0 * fraction * fraction)
    return (
        (3.0 - 2.0 * fraction - root_term) / 8.0,
        (3.0 - 2.0 * fraction + root_term) / 8.0,
        (1.0 + 2.0 * fraction + root_term) / 8.0,
        (1.0 + 2.0 * fraction - root_term) / 8.0,
    )


def pick(distance, weights):
    result = jnp.where(distance == 0, weights[0], 0.0)
    for corner in range(1, CORNERS):
        result = jnp.where(distance == corner, weights[corner], result)
    return result


def wrapped(distance, period):
    if period & (period - 1) == 0:
        return distance & (period - 1)
    return jnp.where(distance < 0, distance + period, distance)


def kernel(
    sizes,
    packed_ref,
    velocity_ref,
    field_ref,
    next_ref,
    markers,
    left,
    right,
    total,
    outgoing,
    incoming,
    z_halo,
    x_halo,
    send_sems,
    recv_sems,
):
    gz_count, col_count, slab_depth, half_x, width_y, rows_each = sizes
    full_x = half_x * col_count
    full_z = slab_depth * gz_count
    group_x = full_x // GROUPS
    local_x = group_x + SUBLANES
    gz = lax.axis_index("gz")
    col = lax.axis_index("col")
    steps = [by for reach in range(1, BAND) for by in (reach, -reach)]

    def gz_at(by):
        return lax.rem(gz + (by + gz_count), gz_count)

    other_col = lax.rem(col + 1, col_count)

    barrier = pltpu.get_barrier_semaphore()
    for by in steps:
        pl.semaphore_signal(barrier, inc=1, device_id={"gz": gz_at(by)}, device_id_type=MESH)
    pl.semaphore_signal(barrier, inc=1, device_id={"col": other_col}, device_id_type=MESH)
    pl.semaphore_wait(barrier, len(steps) + 1)

    copies = []

    def send(source, target, slot, device):
        copy = pltpu.make_async_remote_copy(
            src_ref=source,
            dst_ref=target,
            send_sem=send_sems.at[slot],
            recv_sem=recv_sems.at[slot],
            device_id=device,
            device_id_type=MESH,
        )
        copy.start()
        copies.append(copy)
        return copy

    for slot, by in enumerate(steps):
        send(packed_ref, markers.at[slot + 1], slot + 1, {"gz": gz_at(by)})
    base = len(steps) + 1
    halos = [
        send(velocity_ref.at[slab_depth - 1], z_halo.at[0], base, {"gz": gz_at(1)}),
        send(velocity_ref.at[0], z_halo.at[1], base + 1, {"gz": gz_at(-1)}),
        send(
            velocity_ref.at[:, :, half_x - SUBLANES : half_x],
            x_halo.at[0],
            base + 2,
            {"col": other_col},
        ),
        send(velocity_ref.at[:, :, 0:SUBLANES], x_halo.at[1], base + 3, {"col": other_col}),
    ]

    markers[0] = packed_ref[...]
    total[...] = jnp.zeros_like(total)

    first_x = col * half_x
    first_z = gz * slab_depth
    pieces = rows_each // PIECE_ROWS
    y_rows = [
        (lax.broadcasted_iota(jnp.int32, (2 * SUBLANES, LANES), 0) + start)
        .astype(jnp.float32)
        .astype(jnp.bfloat16)
        for start in range(0, width_y, 2 * SUBLANES)
    ]
    x_rows = lax.broadcasted_iota(jnp.int32, (local_x, LANES), 0)

    def fill(source, piece):
        start = pl.multiple_of(piece * PIECE_ROWS, SUBLANES)

        def param(index):
            return markers[source, pl.ds(index * rows_each + start, PIECE_ROWS), :]

        forces = [param(c) for c in range(3)]
        wx = delta_weights(param(3))
        wy = delta_weights(param(4))
        wz = delta_weights(param(5))
        x_rel = wrapped(param(6).astype(jnp.int32) - first_x, full_x)
        y_cell = param(7)
        targets = []
        for corner in range(CORNERS):
            target = y_cell + corner
            targets.append(jnp.where(target >= width_y, target - width_y, target))
        z_cell = param(8).astype(jnp.int32)
        group = x_rel // group_x
        x_local = x_rel - group * group_x
        members = [jnp.where(group == g, 1.0, 0.0) for g in range(GROUPS)]
        scaled = []
        for plane in range(slab_depth):
            z_weight = pick(wrapped(plane + first_z - z_cell, full_z), wz)
            scaled.extend(z_weight * force for force in forces)
        for row in range(PIECE_ROWS):
            lanes = slice(row * LANES, (row + 1) * LANES)

            def line(value):
                return value[row : row + 1, :]

            def packed_line(value):
                wide = jnp.broadcast_to(line(value), (2 * SUBLANES, LANES))
                return wide.astype(jnp.bfloat16)

            y_targets = [packed_line(target) for target in targets]
            y_weights = [packed_line(w) for w in wy]
            y_members = [packed_line(member) for member in members]
            for part in range(width_y // (2 * SUBLANES)):
                y_row = y_rows[part]
                hits = jnp.zeros((2 * SUBLANES, LANES), jnp.bfloat16)
                for target, weight in zip(y_targets, y_weights):
                    hits = jnp.where(y_row == target, weight, hits)
                for g in range(GROUPS):
                    start_row = g * width_y + part * 2 * SUBLANES
                    right[start_row : start_row + 2 * SUBLANES, lanes] = (hits * y_members[g]).astype(jnp.float32)
            x_hits = pick(x_rows - line(x_local), [line(w) for w in wx])
            for pair in range(len(scaled) // 2):
                both = jnp.concatenate(
                    [line(scaled[2 * pair]) * x_hits, line(scaled[2 * pair + 1]) * x_hits], axis=0
                )
                left[2 * pair * local_x : 2 * (pair + 1) * local_x, lanes] = both

    def one_source(source, _):
        @pl.when(source > 0)
        def _():
            pltpu.make_async_remote_copy(
                src_ref=packed_ref,
                dst_ref=markers.at[source],
                send_sem=send_sems.at[source],
                recv_sem=recv_sems.at[source],
                device_id={"gz": gz_at(1)},
                device_id_type=MESH,
            ).wait_recv()

        def one_piece(piece, _):
            fill(source, piece)
            total[...] += lax.dot_general(
                left[...],
                right[...],
                (((1,), (1,)), ((), ())),
                preferred_element_type=jnp.float32,
            )
            return 0

        lax.fori_loop(0, pieces, one_piece, 0)
        return 0

    lax.fori_loop(0, len(steps) + 1, one_source, 0)

    own_groups = GROUPS // col_count

    def gathered(plane, component, group):
        start = (plane * 3 + component) * local_x
        main = total[start : start + group_x, group * width_y : (group + 1) * width_y]
        before = (group - 1) % GROUPS
        spill = total[
            start + group_x : start + local_x, before * width_y : (before + 1) * width_y
        ]
        return main, spill

    def put(target, plane, component, group, place):
        main, spill = gathered(plane, component, group)
        start = place * group_x
        target[plane, component, start : start + SUBLANES, :] = main[:SUBLANES] + spill
        target[plane, component, start + SUBLANES : start + group_x, :] = main[SUBLANES:]

    for plane in range(slab_depth):
        for component in range(3):
            for place in range(own_groups):
                put(outgoing, plane, component, own_groups + place, place)
    exchange = send(outgoing, incoming, base + 4, {"col": other_col})

    for halo in halos:
        halo.wait_recv()
    x_index = lax.broadcasted_iota(jnp.int32, (half_x, width_y), 0)
    for plane in range(slab_depth):
        for component in range(3):
            for place in range(own_groups):
                put(field_ref, plane, component, place, place)
            here = velocity_ref[plane, component]
            below = z_halo[0, component] if plane == 0 else velocity_ref[plane - 1, component]
            above = (
                z_halo[1, component]
                if plane == slab_depth - 1
                else velocity_ref[plane + 1, component]
            )
            low = x_halo[0, plane, component, SUBLANES - 1 : SUBLANES, :]
            high = x_halo[1, plane, component, 0:1, :]
            x_low = jnp.where(x_index == 0, low, pltpu.roll(here, 1, 0))
            x_high = jnp.where(x_index == half_x - 1, high, pltpu.roll(here, half_x - 1, 0))
            near = above + below + x_low + x_high
            near = near + pltpu.roll(here, 1, 1) + pltpu.roll(here, width_y - 1, 1)
            next_ref[plane, component] = here + VISCOUS * (near - 6.0 * here)

    exchange.wait_recv()
    for plane in range(slab_depth):
        for component in range(3):
            own = field_ref[plane, component] + incoming[plane, component]
            field_ref[plane, component] = own
            next_ref[plane, component] = next_ref[plane, component] + own
    for copy in copies:
        copy.wait_send()


def on_device(sizes, velocity, forces, offsets, cell_x, cell_y, cell_z, band_start):
    gz_count, col_count, slab_depth, half_x, width_y, rows_each = sizes
    full_x = half_x * col_count
    full_z = slab_depth * gz_count
    z_cell = (band_start[0] * slab_depth + cell_z) % full_z
    cells = jnp.stack([cell_x, cell_y, z_cell]).astype(jnp.float32)
    packed = jnp.concatenate([forces, offsets, cells], axis=0).reshape(9 * rows_each, LANES)
    sources = 2 * BAND - 1
    local_x = full_x // GROUPS + SUBLANES
    left_rows = slab_depth * 3 * local_x
    right_rows = GROUPS * width_y
    block = PIECE_ROWS * LANES
    shape = jax.ShapeDtypeStruct(velocity.shape, jnp.float32)
    copies = sources + 5
    return pl.pallas_call(
        functools.partial(kernel, sizes),
        out_shape=(shape, shape),
        in_specs=[pl.BlockSpec(memory_space=pltpu.VMEM)] * 2,
        out_specs=(pl.BlockSpec(memory_space=pltpu.VMEM),) * 2,
        scratch_shapes=[
            pltpu.VMEM((sources, 9 * rows_each, LANES), jnp.float32),
            pltpu.VMEM((left_rows, block), jnp.float32),
            pltpu.VMEM((right_rows, block), jnp.float32),
            pltpu.VMEM((left_rows, right_rows), jnp.float32),
            pltpu.VMEM(velocity.shape, jnp.float32),
            pltpu.VMEM(velocity.shape, jnp.float32),
            pltpu.VMEM((2,) + velocity.shape[1:], jnp.float32),
            pltpu.VMEM((2, slab_depth, 3, SUBLANES, width_y), jnp.float32),
            pltpu.SemaphoreType.DMA((copies,)),
            pltpu.SemaphoreType.DMA((copies,)),
        ],
        compiler_params=pltpu.CompilerParams(
            collective_id=0, has_side_effects=True, vmem_limit_bytes=48 * 1024 * 1024
        ),
    )(packed, velocity)


def solution(mesh):
    from_shapes = functools.partial(sized, mesh)
    in_specs = (
        P("gz", None, "col", None),
        P(None, ("gz", "col")),
        P(None, ("gz", "col")),
        P(("gz", "col")),
        P(("gz", "col")),
        P(("gz", "col")),
        P("gz"),
    )
    out_specs = (P("gz", None, "col", None), P("gz", None, "col", None))
    return jax.shard_map(
        from_shapes, mesh=mesh, in_specs=in_specs, out_specs=out_specs, check_vma=False
    )


def sized(mesh, velocity, forces, offsets, cell_x, cell_y, cell_z, band_start):
    slab_depth, _, half_x, width_y = velocity.shape
    rows_each = cell_x.shape[0] // LANES
    sizes = (mesh.shape["gz"], mesh.shape["col"], slab_depth, half_x, width_y, rows_each)
    return on_device(sizes, velocity, forces, offsets, cell_x, cell_y, cell_z, band_start)
```

```python
import functools

import jax
import jax.numpy as jnp
from jax import lax
from jax.experimental import pallas as pl
from jax.experimental.pallas import tpu as pltpu
from jax.sharding import PartitionSpec as P

BAND = 4
CORNERS = 4
VISCOUS = 0.15
LANES = 128
SUBLANES = 8
PIECE_ROWS = 32
GROUPS = 4
MESH = pl.DeviceIdType.MESH


def delta_weights(fraction):
    root_term = jnp.sqrt(1.0 + 4.0 * fraction - 4.0 * fraction * fraction)
    return (
        (3.0 - 2.0 * fraction - root_term) / 8.0,
        (3.0 - 2.0 * fraction + root_term) / 8.0,
        (1.0 + 2.0 * fraction + root_term) / 8.0,
        (1.0 + 2.0 * fraction - root_term) / 8.0,
    )


def pick(distance, weights):
    result = jnp.where(distance == 0, weights[0], 0.0)
    for corner in range(1, CORNERS):
        result = jnp.where(distance == corner, weights[corner], result)
    return result


def wrapped(distance, period):
    if period & (period - 1) == 0:
        return distance & (period - 1)
    return jnp.where(distance < 0, distance + period, distance)


def kernel(
    sizes,
    packed_ref,
    velocity_ref,
    field_ref,
    next_ref,
    markers,
    left,
    right,
    total,
    outgoing,
    incoming,
    z_halo,
    x_halo,
    send_sems,
    recv_sems,
):
    gz_count, col_count, slab_depth, half_x, width_y, rows_each = sizes
    full_x = half_x * col_count
    full_z = slab_depth * gz_count
    group_x = full_x // GROUPS
    local_x = group_x + SUBLANES
    gz = lax.axis_index("gz")
    col = lax.axis_index("col")
    place_in_band = lax.rem(gz, BAND)
    low_bit, high_bit = lax.rem(place_in_band, 2), place_in_band // 2
    near = [1 - 2 * low_bit, 2 - 4 * high_bit, 3 - 2 * place_in_band]
    far = [by - BAND + 2 * BAND * bit for by, bit in zip(near, (low_bit, high_bit, high_bit))]
    steps = [near[0], near[1], near[2], far[1], far[0], far[2]]
    starts = [0, 0, 1, 2, 2, 3]
    halo_start = 4

    def gz_at(by):
        return lax.rem(gz + (by + gz_count), gz_count)

    other_col = lax.rem(col + 1, col_count)

    barrier = pltpu.get_barrier_semaphore()
    for by in steps:
        pl.semaphore_signal(barrier, inc=1, device_id={"gz": gz_at(by)}, device_id_type=MESH)
    pl.semaphore_signal(barrier, inc=1, device_id={"col": other_col}, device_id_type=MESH)
    pl.semaphore_wait(barrier, len(steps) + 1)

    base = len(steps) + 1

    def remote(source, target, slot, device):
        return pltpu.make_async_remote_copy(
            src_ref=source,
            dst_ref=target,
            send_sem=send_sems.at[slot],
            recv_sem=recv_sems.at[slot],
            device_id=device,
            device_id_type=MESH,
        )

    travels = [
        remote(packed_ref, markers.at[slot + 1], slot + 1, {"gz": gz_at(by)})
        for slot, by in enumerate(steps)
    ]
    halos = [
        remote(velocity_ref.at[slab_depth - 1], z_halo.at[0], base, {"gz": gz_at(1)}),
        remote(velocity_ref.at[0], z_halo.at[1], base + 1, {"gz": gz_at(-1)}),
        remote(
            velocity_ref.at[:, :, half_x - SUBLANES : half_x],
            x_halo.at[0],
            base + 2,
            {"col": other_col},
        ),
        remote(velocity_ref.at[:, :, 0:SUBLANES], x_halo.at[1], base + 3, {"col": other_col}),
    ]
    exchange = remote(outgoing, incoming, base + 4, {"col": other_col})
    for travel, start in zip(travels, starts):
        if start == 0:
            travel.start()

    markers[0] = packed_ref[...]
    total[...] = jnp.zeros_like(total)

    first_x = col * half_x
    first_z = gz * slab_depth
    pieces = rows_each // PIECE_ROWS
    y_rows = [
        (lax.broadcasted_iota(jnp.int32, (2 * SUBLANES, LANES), 0) + start)
        .astype(jnp.float32)
        .astype(jnp.bfloat16)
        for start in range(0, width_y, 2 * SUBLANES)
    ]
    x_rows = lax.broadcasted_iota(jnp.int32, (local_x, LANES), 0)

    def fill(source, piece):
        start = pl.multiple_of(piece * PIECE_ROWS, SUBLANES)

        def param(index):
            return markers[source, pl.ds(index * rows_each + start, PIECE_ROWS), :]

        forces = [param(c) for c in range(3)]
        wx = delta_weights(param(3))
        wy = delta_weights(param(4))
        wz = delta_weights(param(5))
        x_rel = wrapped(param(6).astype(jnp.int32) - first_x, full_x)
        y_cell = param(7)
        targets = []
        for corner in range(CORNERS):
            target = y_cell + corner
            targets.append(jnp.where(target >= width_y, target - width_y, target))
        z_cell = param(8).astype(jnp.int32)
        group = x_rel // group_x
        x_local = x_rel - group * group_x
        members = [jnp.where(group == g, 1.0, 0.0) for g in range(GROUPS)]
        scaled = []
        for plane in range(slab_depth):
            z_weight = pick(wrapped(plane + first_z - z_cell, full_z), wz)
            scaled.extend(z_weight * force for force in forces)
        for row in range(PIECE_ROWS):
            lanes = slice(row * LANES, (row + 1) * LANES)

            def line(value):
                return value[row : row + 1, :]

            def packed_line(value):
                wide = jnp.broadcast_to(line(value), (2 * SUBLANES, LANES))
                return wide.astype(jnp.bfloat16)

            y_targets = [packed_line(target) for target in targets]
            y_weights = [packed_line(w) for w in wy]
            y_members = [packed_line(member) for member in members]
            for part in range(width_y // (2 * SUBLANES)):
                y_row = y_rows[part]
                hits = jnp.zeros((2 * SUBLANES, LANES), jnp.bfloat16)
                for target, weight in zip(y_targets, y_weights):
                    hits = jnp.where(y_row == target, weight, hits)
                for g in range(GROUPS):
                    start_row = g * width_y + part * 2 * SUBLANES
                    right[start_row : start_row + 2 * SUBLANES, lanes] = (hits * y_members[g]).astype(jnp.float32)
            x_hits = pick(x_rows - line(x_local), [line(w) for w in wx])
            for pair in range(len(scaled) // 2):
                both = jnp.concatenate(
                    [line(scaled[2 * pair]) * x_hits, line(scaled[2 * pair + 1]) * x_hits], axis=0
                )
                left[2 * pair * local_x : 2 * (pair + 1) * local_x, lanes] = both

    def one_source(source, _):
        for begin in sorted(set(starts) - {0}):

            @pl.when(source == begin)
            def _():
                for travel, start in zip(travels, starts):
                    if start == begin:
                        travel.start()

        @pl.when(source == halo_start)
        def _():
            for halo in halos:
                halo.start()

        @pl.when(source > 0)
        def _():
            remote(packed_ref, markers.at[source], source, {"gz": gz_at(1)}).wait_recv()

        def one_piece(piece, _):
            fill(source, piece)
            total[...] += lax.dot_general(
                left[...],
                right[...],
                (((1,), (1,)), ((), ())),
                preferred_element_type=jnp.float32,
            )
            return 0

        lax.fori_loop(0, pieces, one_piece, 0)
        return 0

    lax.fori_loop(0, len(steps) + 1, one_source, 0)

    own_groups = GROUPS // col_count

    def gathered(plane, component, group):
        start = (plane * 3 + component) * local_x
        main = total[start : start + group_x, group * width_y : (group + 1) * width_y]
        before = (group - 1) % GROUPS
        spill = total[
            start + group_x : start + local_x, before * width_y : (before + 1) * width_y
        ]
        return main, spill

    def put(target, plane, component, group, place):
        main, spill = gathered(plane, component, group)
        start = place * group_x
        target[plane, component, start : start + SUBLANES, :] = main[:SUBLANES] + spill
        target[plane, component, start + SUBLANES : start + group_x, :] = main[SUBLANES:]

    for plane in range(slab_depth):
        for component in range(3):
            for place in range(own_groups):
                put(outgoing, plane, component, own_groups + place, place)
    exchange.start()

    for halo in halos:
        halo.wait_recv()
    x_index = lax.broadcasted_iota(jnp.int32, (half_x, width_y), 0)
    for plane in range(slab_depth):
        for component in range(3):
            for place in range(own_groups):
                put(field_ref, plane, component, place, place)
            here = velocity_ref[plane, component]
            below = z_halo[0, component] if plane == 0 else velocity_ref[plane - 1, component]
            above = (
                z_halo[1, component]
                if plane == slab_depth - 1
                else velocity_ref[plane + 1, component]
            )
            low = x_halo[0, plane, component, SUBLANES - 1 : SUBLANES, :]
            high = x_halo[1, plane, component, 0:1, :]
            x_low = jnp.where(x_index == 0, low, pltpu.roll(here, 1, 0))
            x_high = jnp.where(x_index == half_x - 1, high, pltpu.roll(here, half_x - 1, 0))
            around = above + below + x_low + x_high
            around = around + pltpu.roll(here, 1, 1) + pltpu.roll(here, width_y - 1, 1)
            next_ref[plane, component] = here + VISCOUS * (around - 6.0 * here)

    exchange.wait_recv()
    for plane in range(slab_depth):
        for component in range(3):
            own = field_ref[plane, component] + incoming[plane, component]
            field_ref[plane, component] = own
            next_ref[plane, component] = next_ref[plane, component] + own
    for copy in travels + halos + [exchange]:
        copy.wait_send()


def on_device(sizes, velocity, forces, offsets, cell_x, cell_y, cell_z, band_start):
    gz_count, col_count, slab_depth, half_x, width_y, rows_each = sizes
    full_x = half_x * col_count
    full_z = slab_depth * gz_count
    z_cell = (band_start[0] * slab_depth + cell_z) % full_z
    cells = jnp.stack([cell_x, cell_y, z_cell]).astype(jnp.float32)
    packed = jnp.concatenate([forces, offsets, cells], axis=0).reshape(9 * rows_each, LANES)
    sources = 2 * BAND - 1
    local_x = full_x // GROUPS + SUBLANES
    left_rows = slab_depth * 3 * local_x
    right_rows = GROUPS * width_y
    block = PIECE_ROWS * LANES
    shape = jax.ShapeDtypeStruct(velocity.shape, jnp.float32)
    copies = sources + 5
    return pl.pallas_call(
        functools.partial(kernel, sizes),
        out_shape=(shape, shape),
        in_specs=[pl.BlockSpec(memory_space=pltpu.VMEM)] * 2,
        out_specs=(pl.BlockSpec(memory_space=pltpu.VMEM),) * 2,
        scratch_shapes=[
            pltpu.VMEM((sources, 9 * rows_each, LANES), jnp.float32),
            pltpu.VMEM((left_rows, block), jnp.float32),
            pltpu.VMEM((right_rows, block), jnp.float32),
            pltpu.VMEM((left_rows, right_rows), jnp.float32),
            pltpu.VMEM(velocity.shape, jnp.float32),
            pltpu.VMEM(velocity.shape, jnp.float32),
            pltpu.VMEM((2,) + velocity.shape[1:], jnp.float32),
            pltpu.VMEM((2, slab_depth, 3, SUBLANES, width_y), jnp.float32),
            pltpu.SemaphoreType.DMA((copies,)),
            pltpu.SemaphoreType.DMA((copies,)),
        ],
        compiler_params=pltpu.CompilerParams(
            collective_id=0, has_side_effects=True, vmem_limit_bytes=48 * 1024 * 1024
        ),
    )(packed, velocity)


def solution(mesh):
    from_shapes = functools.partial(sized, mesh)
    in_specs = (
        P("gz", None, "col", None),
        P(None, ("gz", "col")),
        P(None, ("gz", "col")),
        P(("gz", "col")),
        P(("gz", "col")),
        P(("gz", "col")),
        P("gz"),
    )
    out_specs = (P("gz", None, "col", None), P("gz", None, "col", None))
    return jax.shard_map(
        from_shapes, mesh=mesh, in_specs=in_specs, out_specs=out_specs, check_vma=False
    )


def sized(mesh, velocity, forces, offsets, cell_x, cell_y, cell_z, band_start):
    slab_depth, _, half_x, width_y = velocity.shape
    rows_each = cell_x.shape[0] // LANES
    sizes = (mesh.shape["gz"], mesh.shape["col"], slab_depth, half_x, width_y, rows_each)
    return on_device(sizes, velocity, forces, offsets, cell_x, cell_y, cell_z, band_start)
```

```python
import functools

import jax
import jax.numpy as jnp
from jax import lax
from jax.experimental import pallas as pl
from jax.experimental.pallas import tpu as pltpu
from jax.sharding import PartitionSpec as P

BAND = 4
CORNERS = 4
VISCOUS = 0.15
LANES = 128
SUBLANES = 8
PIECE_ROWS = 32
GROUPS = 4
MESH = pl.DeviceIdType.MESH


def delta_weights(fraction):
    root_term = jnp.sqrt(1.0 + 4.0 * fraction - 4.0 * fraction * fraction)
    return (
        (3.0 - 2.0 * fraction - root_term) / 8.0,
        (3.0 - 2.0 * fraction + root_term) / 8.0,
        (1.0 + 2.0 * fraction + root_term) / 8.0,
        (1.0 + 2.0 * fraction - root_term) / 8.0,
    )


def pick(distance, weights):
    result = jnp.where(distance == 0, weights[0], 0.0)
    for corner in range(1, CORNERS):
        result = jnp.where(distance == corner, weights[corner], result)
    return result


def wrapped(distance, period):
    if period & (period - 1) == 0:
        return distance & (period - 1)
    return jnp.where(distance < 0, distance + period, distance)


def kernel(
    sizes,
    packed_ref,
    velocity_hbm,
    field_ref,
    next_ref,
    markers,
    left,
    right,
    total,
    outgoing,
    incoming,
    z_halo,
    x_halo,
    velocity_ref,
    load_sem,
    send_sems,
    recv_sems,
):
    gz_count, col_count, slab_depth, half_x, width_y, rows_each = sizes
    full_x = half_x * col_count
    full_z = slab_depth * gz_count
    group_x = full_x // GROUPS
    main_rows = slab_depth * 3 * group_x
    gz = lax.axis_index("gz")
    col = lax.axis_index("col")
    place_in_band = lax.rem(gz, BAND)
    low_bit, high_bit = lax.rem(place_in_band, 2), place_in_band // 2
    near = [1 - 2 * low_bit, 2 - 4 * high_bit, 3 - 2 * place_in_band]
    far = [by - BAND + 2 * BAND * bit for by, bit in zip(near, (low_bit, high_bit, high_bit))]
    steps = [near[0], near[1], near[2], far[1], far[0], far[2]]
    starts = [0, 0, 1, 2, 2, 3]
    halo_start = 4

    def gz_at(by):
        return lax.rem(gz + (by + gz_count), gz_count)

    other_col = lax.rem(col + 1, col_count)

    barrier = pltpu.get_barrier_semaphore()
    for by in steps:
        pl.semaphore_signal(barrier, inc=1, device_id={"gz": gz_at(by)}, device_id_type=MESH)
    pl.semaphore_signal(barrier, inc=1, device_id={"col": other_col}, device_id_type=MESH)
    pl.semaphore_wait(barrier, len(steps) + 1)

    base = len(steps) + 1

    def remote(source, target, slot, device):
        return pltpu.make_async_remote_copy(
            src_ref=source,
            dst_ref=target,
            send_sem=send_sems.at[slot],
            recv_sem=recv_sems.at[slot],
            device_id=device,
            device_id_type=MESH,
        )

    travels = [
        remote(packed_ref, markers.at[slot + 1], slot + 1, {"gz": gz_at(by)})
        for slot, by in enumerate(steps)
    ]
    halos = [
        remote(velocity_ref.at[slab_depth - 1], z_halo.at[0], base, {"gz": gz_at(1)}),
        remote(velocity_ref.at[0], z_halo.at[1], base + 1, {"gz": gz_at(-1)}),
        remote(
            velocity_ref.at[:, :, half_x - SUBLANES : half_x],
            x_halo.at[0],
            base + 2,
            {"col": other_col},
        ),
        remote(velocity_ref.at[:, :, 0:SUBLANES], x_halo.at[1], base + 3, {"col": other_col}),
    ]
    exchange = remote(outgoing, incoming, base + 4, {"col": other_col})
    for travel, start in zip(travels, starts):
        if start == 0:
            travel.start()

    load = pltpu.make_async_copy(velocity_hbm, velocity_ref, load_sem)
    load.start()
    markers[0] = packed_ref[...]
    total[...] = jnp.zeros_like(total)

    first_x = col * half_x
    first_z = gz * slab_depth
    pieces = rows_each // PIECE_ROWS
    y_rows = [
        (lax.broadcasted_iota(jnp.int32, (2 * SUBLANES, LANES), 0) + start)
        .astype(jnp.float32)
        .astype(jnp.bfloat16)
        for start in range(0, width_y, 2 * SUBLANES)
    ]
    x_rows = lax.broadcasted_iota(jnp.int32, (group_x, LANES), 0)
    eight = lax.broadcasted_iota(jnp.int32, (SUBLANES, LANES), 0)
    first_half = eight < CORNERS
    spill_rows = group_x + jnp.where(first_half, eight, eight - CORNERS)

    def fill(source, piece):
        start = pl.multiple_of(piece * PIECE_ROWS, SUBLANES)

        def param(index):
            return markers[source, pl.ds(index * rows_each + start, PIECE_ROWS), :]

        forces = [param(c) for c in range(3)]
        wx = delta_weights(param(3))
        wy = delta_weights(param(4))
        wz = delta_weights(param(5))
        x_rel = wrapped(param(6).astype(jnp.int32) - first_x, full_x)
        y_cell = param(7)
        targets = []
        for corner in range(CORNERS):
            target = y_cell + corner
            targets.append(jnp.where(target >= width_y, target - width_y, target))
        z_cell = param(8).astype(jnp.int32)
        group = x_rel // group_x
        x_local = x_rel - group * group_x
        members = [jnp.where(group == g, 1.0, 0.0) for g in range(GROUPS)]
        scaled = []
        for plane in range(slab_depth):
            z_weight = pick(wrapped(plane + first_z - z_cell, full_z), wz)
            scaled.extend(z_weight * force for force in forces)
        for row in range(PIECE_ROWS):
            lanes = slice(row * LANES, (row + 1) * LANES)

            def line(value):
                return value[row : row + 1, :]

            def packed_line(value):
                wide = jnp.broadcast_to(line(value), (2 * SUBLANES, LANES))
                return wide.astype(jnp.bfloat16)

            y_targets = [packed_line(target) for target in targets]
            y_weights = [packed_line(w) for w in wy]
            y_members = [packed_line(member) for member in members]
            for part in range(width_y // (2 * SUBLANES)):
                y_row = y_rows[part]
                hits = jnp.zeros((2 * SUBLANES, LANES), jnp.bfloat16)
                for target, weight in zip(y_targets, y_weights):
                    hits = jnp.where(y_row == target, weight, hits)
                for g in range(GROUPS):
                    start_row = g * width_y + part * 2 * SUBLANES
                    right[start_row : start_row + 2 * SUBLANES, lanes] = (hits * y_members[g]).astype(jnp.float32)
            x_weights = [line(w) for w in wx]
            x_hits = pick(x_rows - line(x_local), x_weights)
            spill_hits = pick(spill_rows - line(x_local), x_weights)
            for index, value in enumerate(scaled):
                left[index * group_x : (index + 1) * group_x, lanes] = line(value) * x_hits
            for pair in range(len(scaled) // 2):
                both = jnp.where(first_half, line(scaled[2 * pair]), line(scaled[2 * pair + 1]))
                start_row = main_rows + pair * SUBLANES
                left[start_row : start_row + SUBLANES, lanes] = both * spill_hits

    def one_source(source, _):
        for begin in sorted(set(starts) - {0}):

            @pl.when(source == begin)
            def _():
                for travel, start in zip(travels, starts):
                    if start == begin:
                        travel.start()

        @pl.when(source == halo_start)
        def _():
            load.wait()
            for halo in halos:
                halo.start()

        @pl.when(source > 0)
        def _():
            remote(packed_ref, markers.at[source], source, {"gz": gz_at(1)}).wait_recv()

        def one_piece(piece, _):
            fill(source, piece)
            total[...] += lax.dot_general(
                left[...],
                right[...],
                (((1,), (1,)), ((), ())),
                preferred_element_type=jnp.float32,
            )
            return 0

        lax.fori_loop(0, pieces, one_piece, 0)
        return 0

    lax.fori_loop(0, len(steps) + 1, one_source, 0)

    own_groups = GROUPS // col_count

    spill_keep = lax.broadcasted_iota(jnp.int32, (SUBLANES, width_y), 0) < CORNERS

    def gathered(plane, component, group):
        index = plane * 3 + component
        start = index * group_x
        main = total[start : start + group_x, group * width_y : (group + 1) * width_y]
        before = (group - 1) % GROUPS
        start = main_rows + index // 2 * SUBLANES
        spill = total[start : start + SUBLANES, before * width_y : (before + 1) * width_y]
        if index % 2 == 1:
            spill = pltpu.roll(spill, CORNERS, 0)
        spill = jnp.where(spill_keep, spill, 0.0)
        return main, spill

    def put(target, plane, component, group, place):
        main, spill = gathered(plane, component, group)
        start = place * group_x
        target[plane, component, start : start + SUBLANES, :] = main[:SUBLANES] + spill
        target[plane, component, start + SUBLANES : start + group_x, :] = main[SUBLANES:]

    for plane in range(slab_depth):
        for component in range(3):
            for place in range(own_groups):
                put(outgoing, plane, component, own_groups + place, place)
    exchange.start()

    for halo in halos:
        halo.wait_recv()
    x_index = lax.broadcasted_iota(jnp.int32, (half_x, width_y), 0)
    for plane in range(slab_depth):
        for component in range(3):
            for place in range(own_groups):
                put(field_ref, plane, component, place, place)
            here = velocity_ref[plane, component]
            below = z_halo[0, component] if plane == 0 else velocity_ref[plane - 1, component]
            above = (
                z_halo[1, component]
                if plane == slab_depth - 1
                else velocity_ref[plane + 1, component]
            )
            low = x_halo[0, plane, component, SUBLANES - 1 : SUBLANES, :]
            high = x_halo[1, plane, component, 0:1, :]
            x_low = jnp.where(x_index == 0, low, pltpu.roll(here, 1, 0))
            x_high = jnp.where(x_index == half_x - 1, high, pltpu.roll(here, half_x - 1, 0))
            around = above + below + x_low + x_high
            around = around + pltpu.roll(here, 1, 1) + pltpu.roll(here, width_y - 1, 1)
            next_ref[plane, component] = here + VISCOUS * (around - 6.0 * here)

    exchange.wait_recv()
    for plane in range(slab_depth):
        for component in range(3):
            own = field_ref[plane, component] + incoming[plane, component]
            field_ref[plane, component] = own
            next_ref[plane, component] = next_ref[plane, component] + own
    for copy in travels + halos + [exchange]:
        copy.wait_send()


def on_device(sizes, velocity, forces, offsets, cell_x, cell_y, cell_z, band_start):
    gz_count, col_count, slab_depth, half_x, width_y, rows_each = sizes
    full_x = half_x * col_count
    full_z = slab_depth * gz_count
    z_cell = (band_start[0] * slab_depth + cell_z) % full_z
    cells = jnp.stack([cell_x, cell_y, z_cell]).astype(jnp.float32)
    packed = jnp.concatenate([forces, offsets, cells], axis=0).reshape(9 * rows_each, LANES)
    sources = 2 * BAND - 1
    group_x = full_x // GROUPS
    left_rows = slab_depth * 3 * group_x + (slab_depth * 3 + 1) // 2 * SUBLANES
    right_rows = GROUPS * width_y
    block = PIECE_ROWS * LANES
    shape = jax.ShapeDtypeStruct(velocity.shape, jnp.float32)
    copies = sources + 5
    return pl.pallas_call(
        functools.partial(kernel, sizes),
        out_shape=(shape, shape),
        in_specs=[pl.BlockSpec(memory_space=pltpu.VMEM), pl.BlockSpec(memory_space=pl.ANY)],
        out_specs=(pl.BlockSpec(memory_space=pltpu.VMEM),) * 2,
        scratch_shapes=[
            pltpu.VMEM((sources, 9 * rows_each, LANES), jnp.float32),
            pltpu.VMEM((left_rows, block), jnp.float32),
            pltpu.VMEM((right_rows, block), jnp.float32),
            pltpu.VMEM((left_rows, right_rows), jnp.float32),
            pltpu.VMEM(velocity.shape, jnp.float32),
            pltpu.VMEM(velocity.shape, jnp.float32),
            pltpu.VMEM((2,) + velocity.shape[1:], jnp.float32),
            pltpu.VMEM((2, slab_depth, 3, SUBLANES, width_y), jnp.float32),
            pltpu.VMEM(velocity.shape, jnp.float32),
            pltpu.SemaphoreType.DMA,
            pltpu.SemaphoreType.DMA((copies,)),
            pltpu.SemaphoreType.DMA((copies,)),
        ],
        compiler_params=pltpu.CompilerParams(
            collective_id=0, has_side_effects=True, vmem_limit_bytes=48 * 1024 * 1024
        ),
    )(packed, velocity)


def solution(mesh):
    from_shapes = functools.partial(sized, mesh)
    in_specs = (
        P("gz", None, "col", None),
        P(None, ("gz", "col")),
        P(None, ("gz", "col")),
        P(("gz", "col")),
        P(("gz", "col")),
        P(("gz", "col")),
        P("gz"),
    )
    out_specs = (P("gz", None, "col", None), P("gz", None, "col", None))
    return jax.shard_map(
        from_shapes, mesh=mesh, in_specs=in_specs, out_specs=out_specs, check_vma=False
    )


def sized(mesh, velocity, forces, offsets, cell_x, cell_y, cell_z, band_start):
    slab_depth, _, half_x, width_y = velocity.shape
    rows_each = cell_x.shape[0] // LANES
    sizes = (mesh.shape["gz"], mesh.shape["col"], slab_depth, half_x, width_y, rows_each)
    return on_device(sizes, velocity, forces, offsets, cell_x, cell_y, cell_z, band_start)
```
